32 devices in a mesh: blk: 8 (over y, x, core), grp: 4 (over z).
Axes of the slice: x: 2, y: 2, z: 4, core: 2. Of those that a mesh axis runs over, the one named last changes fastest.
Arguments:
- depth: float32 [256, 128, 128], P(('blk', 'grp')), may hold values from 0.2 to 1
- cell_dx: float32 [256, 128, 128], P(('blk', 'grp')), may hold values from 0.6 to 1.5
- cell_dy: float32 [256, 128, 128], P(('blk', 'grp')), may hold values from 0.6 to 1.5
- forcing: float32 [256, 128, 128], P(('blk', 'grp')), may hold values from -6 to 6
- land_mask: int32 [256, 128, 128], P(('blk', 'grp')), may hold values 0 or 1
- dest_block: int32 [256], P(('blk', 'grp')), may hold values from -1 to 127, as said below
- source_slot: int32 [128], P(('blk', 'grp')), may hold values from 0 to 255, as said below
- neighbours: int32 [128, 8], P(('blk', 'grp')), may hold values from -1 to 127, as said below
Outputs:
- solution: float32 [128, 128, 128], P(('blk', 'grp'))
- residual: float32 [128, 128, 128], P(('blk', 'grp'))
The draws below stay inside these ranges and needn't reach their ends.
Inputs may be any that keep to these rules, and one draw needn't show every extreme that they name: `dest_block`: every ocean block is held by exactly one old slot; a block's old and new owners share their index on grp and lie in the same aligned group of four indices on blk. One device's live slots send at most 4 blocks to any one device; in every band some devices hold no block and some have all 8 slots live. `source_slot`: the inverse of dest_block. North and south neighbours lie on devices with the same index on grp; east, north-east and south-east neighbours on the device with the same index on blk and the next index on grp, cyclically; west, north-west and south-west ones on the previous index on grp.
All inputs are finite; a program needn't handle non-finite values. No bound on the sum of `land_mask` on one device may be relied on, other than what follows from the above.
Results may differ from the reference program's by a relative error of at most 0.000034.
Values sent between devices are 32-bit elements; how exact they have to be, the bound alone decides.
A program may use at most 64 MiB of HBM per device.

```python
import math
import jax
import jax.numpy as jnp

SIDE = 128
BX = 128
BLK_DEV = 4
SWEEPS = 4
CAP = 8
NB = 128
SLOTS = 256
N_BLK = 8
N_GRP = 4


def move_plan(count):
    new_list = []
    old_list = []
    rank_list = []
    within_list = []
    taken = [0, 0, 0, 0]
    for target in range(4):
        for within in range(count):
            if target == 1:
                anchor = 0
            elif target == 0:
                anchor = 3 if within == 0 else 0
            elif target == 2:
                anchor = 3 if within == 0 else 2
            else:
                anchor = 0 if within == 0 else 2 if within == 1 else 3
            new_list.append(target)
            old_list.append(anchor)
            rank_list.append(taken[anchor])
            within_list.append(within)
            taken[anchor] = taken[anchor] + 1
    return (new_list, old_list, rank_list, within_list)


def block_layout(key):
    base = jax.random.fold_in(key, 11)
    windows = N_BLK // 4
    new_list, old_list, rank_list, within_list = move_plan(BLK_DEV)
    new_pos = jnp.array(new_list, dtype=jnp.int32)[None, None, :]
    old_pos = jnp.array(old_list, dtype=jnp.int32)[None, None, :]
    ranks = jnp.array(rank_list, dtype=jnp.int32)[None, None, :]
    within = jnp.array(within_list, dtype=jnp.int32)[None, None, :]
    masks = jax.random.randint(jax.random.fold_in(base, 1), (N_GRP, windows, 1), 0, 4, dtype=jnp.int32)
    window_base = 4 * jnp.arange(windows, dtype=jnp.int32)[None, :, None]
    new_owner = window_base + jnp.bitwise_xor(new_pos, masks)
    old_owner = window_base + jnp.bitwise_xor(old_pos, masks)
    slot_keys = jax.random.split(jax.random.fold_in(base, 3), N_BLK * N_GRP)
    orders = jax.vmap(lambda one_key: jax.random.permutation(one_key, CAP))(slot_keys).astype(jnp.int32).reshape(N_BLK, N_GRP, CAP)
    shape = (N_GRP, windows, 4 * BLK_DEV)
    band_full = jnp.broadcast_to(jnp.arange(N_GRP, dtype=jnp.int32)[:, None, None], shape)
    within_full = jnp.broadcast_to(within, shape)
    rank_full = jnp.broadcast_to(ranks, shape)
    slot_old = orders[old_owner, band_full, rank_full]
    new_id = ((new_owner * N_GRP + band_full) * BLK_DEV + within_full).reshape(-1).astype(jnp.int32)
    old_id = ((old_owner * N_GRP + band_full) * CAP + slot_old).reshape(-1).astype(jnp.int32)
    source = jnp.zeros((NB,), jnp.int32).at[new_id].set(old_id)
    dest = jnp.full((SLOTS,), -1, jnp.int32).at[old_id].set(new_id)
    return (source, dest)


def draw_source_slot(key, part):
    return block_layout(key)[0]


def draw_dest_block(key, part):
    return block_layout(key)[1]


def draw_neighbours(key, part):
    base = jax.random.fold_in(key, 23)
    owner_new = jnp.arange(N_BLK, dtype=jnp.int32)[:, None, None, None]
    band = jnp.arange(N_GRP, dtype=jnp.int32)[None, :, None, None]
    shape = (N_BLK, N_GRP, BLK_DEV, 8)
    far_owner = jax.random.randint(jax.random.fold_in(base, 1), shape, 0, N_BLK, dtype=jnp.int32)
    far_slot = jax.random.randint(jax.random.fold_in(base, 2), shape, 0, BLK_DEV, dtype=jnp.int32)
    gaps = jax.random.randint(jax.random.fold_in(base, 3), shape, 0, 5, dtype=jnp.int32)
    east_band = (band + 1) % N_GRP
    west_band = (band + N_GRP - 1) % N_GRP
    polar = (far_owner * N_GRP + band) * BLK_DEV + far_slot
    eastern = (owner_new * N_GRP + east_band) * BLK_DEV + far_slot
    western = (owner_new * N_GRP + west_band) * BLK_DEV + far_slot
    ids = jnp.stack((polar[..., 0], polar[..., 1], eastern[..., 2], western[..., 3], eastern[..., 4], western[..., 5], eastern[..., 6], western[..., 7]), axis=-1)
    ids = jnp.where(gaps == 0, -1, ids)
    return ids.reshape(NB, 8).astype(jnp.int32)


def plant(values, key, smallest, high):
    longest = values.shape.index(max(values.shape))
    spots = []
    for shift in (0, 1):
        where = [jax.random.randint(jax.random.fold_in(key, axis), (), 0, length) for axis, length in enumerate(values.shape)]
        where[longest] = (where[longest] + shift) % values.shape[longest]
        spots.append(tuple(where))
    return values.at[spots[0]].set(smallest).at[spots[1]].set(high)


def steps_of(own_key, dims, cuts, smallest, top_value):
    level, own = 1.0, jax.random.fold_in(own_key, 6)
    for axis_at, blocks in cuts:
        heights = jnp.exp(jax.random.uniform(jax.random.fold_in(own, axis_at), (blocks,), jnp.float32, smallest / len(cuts), top_value / len(cuts)))
        level = level * jnp.repeat(heights, dims[axis_at] // blocks).reshape([-1 if axis == axis_at else 1 for axis in range(len(dims))])
    return level


def gaussian(stream_key, shape, spread, bound, cuts=(), kind=jnp.bfloat16):
    factor_of = steps_of(stream_key, shape, cuts, -0.22, 0.18) if cuts else 1.0
    drawn = jax.random.normal(stream_key, shape, jnp.float32) * spread * factor_of
    return jnp.minimum(jnp.maximum(drawn, -bound), bound).astype(kind)


def setup_inputs(seed: int = 0) -> dict:
    keys = jax.random.split(jax.random.key(seed), 9)
    depth = jnp.clip(0.2 + 0.8 * jax.random.uniform(keys[0], (SLOTS, BX, SIDE), jnp.float32) ** steps_of(keys[0], (SLOTS, BX, SIDE), ((0, 32),), -0.2, 0.2), 0.2, 1.0)
    cell_dx = jnp.clip(jnp.exp(math.log(1.5) - 0.9162907 * jax.random.uniform(keys[1], (SLOTS, BX, SIDE), jnp.float32) ** steps_of(keys[1], (SLOTS, BX, SIDE), ((0, 32),), -0.2, 0.2)), 0.6, 1.5)
    cell_dy = jnp.clip(jnp.exp(math.log(1.5) - 0.9162907 * jax.random.uniform(keys[2], (SLOTS, BX, SIDE), jnp.float32) ** steps_of(keys[2], (SLOTS, BX, SIDE), ((0, 32),), -0.2, 0.2)), 0.6, 1.5)
    forcing = gaussian(keys[3], (SLOTS, BX, SIDE), 1.0, 6.0, ((0, 32),), jnp.float32)
    land_mask = plant((jax.random.randint(keys[4], (SLOTS, BX, SIDE), 0, 5) < 4).astype(jnp.int32), jax.random.fold_in(keys[4], 1), 0, 1)
    dest_block = draw_dest_block(jax.random.fold_in(keys[8], 71), 0)
    source_slot = draw_source_slot(jax.random.fold_in(keys[8], 71), 0)
    neighbours = draw_neighbours(jax.random.fold_in(keys[8], 71), 0)
    return {"depth": depth, "cell_dx": cell_dx, "cell_dy": cell_dy, "forcing": forcing, "land_mask": land_mask, "dest_block": dest_block, "source_slot": source_slot, "neighbours": neighbours}


tau_mass = 6.0
low_bound = 0.2
high_bound = 1.9


def coefficients(ocean_depth, cell_dx, cell_dy):
    ratio_x = cell_dy / cell_dx
    ratio_y = cell_dx / cell_dy
    coef_x = ocean_depth * ratio_x
    coef_y = ocean_depth * ratio_y
    coef_c = 0.125 * ocean_depth * (ratio_x + ratio_y)
    coef_d = 2.0 * coef_x + 2.0 * coef_y + 4.0 * coef_c + tau_mass * cell_dx * cell_dy
    return coef_x, coef_y, coef_c, coef_d


def combine(iterate, coefs, north_row, south_row, west_col, east_col, north_west, north_east, south_west, south_east):
    coef_x, coef_y, coef_c, coef_d = coefs
    top_pad = jnp.concatenate((north_west[:, None], north_row, north_east[:, None]), axis=1)
    bottom_pad = jnp.concatenate((south_west[:, None], south_row, south_east[:, None]), axis=1)
    middle = jnp.concatenate((west_col[:, :, None], iterate, east_col[:, :, None]), axis=2)
    padded = jnp.concatenate((top_pad[:, None, :], middle, bottom_pad[:, None, :]), axis=1)
    from_north = padded[:, :-2, 1:-1]
    from_south = padded[:, 2:, 1:-1]
    from_west = padded[:, 1:-1, :-2]
    from_east = padded[:, 1:-1, 2:]
    diagonal = padded[:, :-2, :-2] + padded[:, :-2, 2:] + padded[:, 2:, :-2] + padded[:, 2:, 2:]
    return coef_d * iterate - coef_x * (from_east + from_west) - coef_y * (from_north + from_south) - coef_c * diagonal


def apply_operator(iterate, coefs, neighbours):
    present = neighbours >= 0
    safe_ids = jnp.where(present, neighbours, 0).astype(jnp.int32)
    top_rows = iterate[:, 0, :]
    bottom_rows = iterate[:, -1, :]
    left_cols = iterate[:, :, 0]
    right_cols = iterate[:, :, -1]
    north_row = jnp.where(present[:, 0, None], bottom_rows[safe_ids[:, 0]], 0.0)
    south_row = jnp.where(present[:, 1, None], top_rows[safe_ids[:, 1]], 0.0)
    east_col = jnp.where(present[:, 2, None], left_cols[safe_ids[:, 2]], 0.0)
    west_col = jnp.where(present[:, 3, None], right_cols[safe_ids[:, 3]], 0.0)
    north_east = jnp.where(present[:, 4], bottom_rows[safe_ids[:, 4], 0], 0.0)
    north_west = jnp.where(present[:, 5], bottom_rows[safe_ids[:, 5], -1], 0.0)
    south_east = jnp.where(present[:, 6], top_rows[safe_ids[:, 6], 0], 0.0)
    south_west = jnp.where(present[:, 7], top_rows[safe_ids[:, 7], -1], 0.0)
    return combine(iterate, coefs, north_row, south_row, west_col, east_col, north_west, north_east, south_west, south_east)


def reference(depth, cell_dx, cell_dy, forcing, land_mask, dest_block, source_slot, neighbours):
    ocean_mask = land_mask.astype(depth.dtype)
    ocean_depth = depth * ocean_mask
    source_old = forcing * ocean_mask
    old_coefs = coefficients(ocean_depth, cell_dx, cell_dy)
    coefs = tuple(field[source_slot] for field in old_coefs)
    target = jnp.where(dest_block >= 0, dest_block, NB).astype(jnp.int32)
    source = jnp.zeros((NB, BX, SIDE), depth.dtype).at[target].set(source_old, mode="drop")
    coef_d = coefs[3]
    scale_alpha = 2.0 / (high_bound - low_bound)
    scale_beta = (high_bound + low_bound) / (high_bound - low_bound)
    scale_gamma = scale_beta / scale_alpha
    relax_weight = 2.0 / scale_gamma
    update = source / (scale_gamma * coef_d)
    solution = update
    residual = source - apply_operator(solution, coefs, neighbours)
    for sweep in range(SWEEPS - 1):
        relax_weight = 1.0 / (scale_gamma - relax_weight / (4.0 * scale_alpha ** 2))
        update = relax_weight * residual / coef_d + (scale_gamma * relax_weight - 1.0) * update
        solution = solution + update
        residual = source - apply_operator(solution, coefs, neighbours)
    return solution, residual
```

```python
import functools

import jax
import jax.numpy as jnp
from jax import lax
from jax.experimental import pallas as pl
from jax.experimental.pallas import tpu as pltpu
from jax.sharding import PartitionSpec as P

SWEEPS = 4
TAU_MASS = 6.0
LOW_BOUND = 0.2
HIGH_BOUND = 1.9
CHUNK = 32
PAD = 8
MESH = pl.DeviceIdType.MESH
EXACT = lax.Precision.HIGHEST


def relax_weights():
    alpha = 2.0 / (HIGH_BOUND - LOW_BOUND)
    beta = (HIGH_BOUND + LOW_BOUND) / (HIGH_BOUND - LOW_BOUND)
    gamma = beta / alpha
    weight = 2.0 / gamma
    weights = []
    for _ in range(SWEEPS - 1):
        weight = 1.0 / (gamma - weight / (4.0 * alpha**2))
        weights.append((weight, gamma * weight - 1.0))
    return gamma, weights


def kernel(
    owners,
    bands,
    depth_hbm,
    dx_hbm,
    dy_hbm,
    forcing_hbm,
    mask_hbm,
    dest_smem,
    dest_row,
    neigh,
    sol_out,
    res_out,
    depth_v,
    dx_v,
    dy_v,
    forcing_v,
    mask_v,
    coef_x,
    coef_y,
    coef_d,
    inv_d,
    source,
    update,
    field,
    resid,
    table,
    band_tables,
    side_tables,
    pick_rows,
    pick_cols,
    edge_rows,
    edge_cols,
    band_rows,
    side_cols,
    col_tile,
    turned,
    halo_cols,
    find,
    have,
    half_out,
    half_in,
    pair_out,
    pair_in,
    cross_out,
    cross_in,
    load_sems,
    row_send,
    row_recv,
    col_send,
    col_recv,
    move_send,
    move_recv,
):
    slots, height, width = depth_v.shape
    blocks = neigh.shape[0]
    me = lax.axis_index("blk")
    band = lax.axis_index("grp")
    core = me % 2
    sibling = me + 1 - 2 * core
    base = me - me % 4
    inner = me % 4
    east_band = (band + 1) % bands
    west_band = (band + bands - 1) % bands
    half = height // 2

    loads = [
        pltpu.make_async_copy(src, dst, load_sems.at[i])
        for i, (src, dst) in enumerate(
            (
                (dx_hbm, dx_v),
                (dy_hbm, dy_v),
                (depth_hbm, depth_v),
                (mask_hbm, mask_v),
                (forcing_hbm, forcing_v),
            )
        )
    ]
    for load in loads:
        load.start()

    barrier = pltpu.get_barrier_semaphore()
    for step in range(1, owners):
        pl.semaphore_signal(
            barrier, inc=1, device_id=((me + step) % owners, band), device_id_type=MESH
        )
    for step in range(4):
        for side in (east_band, west_band):
            pl.semaphore_signal(
                barrier,
                inc=1,
                device_id=(base + (inner + step) % 4, side),
                device_id_type=MESH,
            )

    table[...] = jnp.zeros_like(table)
    table[0:blocks, 0:8] = (neigh[...] + 1).astype(jnp.float32)
    table[blocks : blocks + 1, 0:slots] = (dest_row[...] + 1).astype(jnp.float32)
    band_tables[0] = table[...]

    targets = (me, sibling, (base + (inner + 2) % 4), (base + (sibling % 4 + 2) % 4))
    for t, target in enumerate(targets):
        for j in range(blocks):
            wanted = (target * bands + band) * blocks + j
            place = jnp.int32(0)
            count = jnp.int32(0)
            for s in range(slots):
                hit = dest_smem[s] == wanted
                place = jnp.where(hit, s, place)
                count = jnp.where(hit, 1, count)
            find[t * blocks + j] = place
            have[t * blocks + j] = count.astype(jnp.float32)

    gamma, weights = relax_weights()
    lane = lax.broadcasted_iota(jnp.int32, (CHUNK, width), 1)
    first_lane = lane == 0
    last_lane = lane == width - 1
    pair = lane // 2

    def put_columns(s, r0, value):
        moved = pltpu.roll(value, 2 * s + 1, 1)
        rows = pl.ds(r0, CHUNK)
        col_tile[rows, :] = jnp.where(pair == s, moved, col_tile[rows, :])

    col_tile[...] = jnp.zeros_like(col_tile)
    for load in loads:
        load.wait()

    def prepare(s, carry):
        for r0 in range(0, height, CHUNK):
            rows = pl.ds(r0, CHUNK)
            ocean = mask_v[s, rows, :].astype(jnp.float32)
            dx = dx_v[s, rows, :]
            dy = dy_v[s, rows, :]
            area = dx * dy
            scaled = depth_v[s, rows, :] * ocean / area
            cx = scaled * (dy * dy)
            cy = scaled * (dx * dx)
            cd = 2.5 * (cx + cy) + TAU_MASS * area
            inv = 1.0 / cd
            src = forcing_v[s, rows, :] * ocean
            start = src * (inv * (1.0 / gamma))
            coef_x[s, rows, :] = cx
            coef_y[s, rows, :] = cy
            coef_d[s, rows, :] = cd
            inv_d[s, rows, :] = inv
            source[s, rows, :] = src
            update[s, rows, :] = start
            field[0, s, pl.ds(PAD + r0, CHUNK), :] = start
            put_columns(s, r0, start)
        return carry

    lax.fori_loop(0, slots, prepare, 0)

    def send_tables():
        for step in range(1, owners):
            pltpu.make_async_remote_copy(
                src_ref=table,
                dst_ref=band_tables.at[owners - step],
                send_sem=row_send.at[SWEEPS],
                recv_sem=row_recv.at[SWEEPS],
                device_id=((me + step) % owners, band),
                device_id_type=MESH,
            ).start()
        for step in range(4):
            for slot, side in ((step, west_band), (4 + step, east_band)):
                pltpu.make_async_remote_copy(
                    src_ref=table,
                    dst_ref=side_tables.at[slot],
                    send_sem=col_send.at[SWEEPS],
                    recv_sem=col_recv.at[SWEEPS],
                    device_id=(base + (inner + step) % 4, side),
                    device_id_type=MESH,
                ).start()

    def send_edges(k):
        now = k % 2
        for s in range(slots):
            edge_rows[k, s : s + 1, :] = field[now, s, PAD : PAD + 1, :]
            edge_rows[k, slots + s : slots + s + 1, :] = field[
                now, s, PAD + height - 1 : PAD + height, :
            ]
        for step in range(1, owners):
            pltpu.make_async_remote_copy(
                src_ref=edge_rows.at[k],
                dst_ref=band_rows.at[k, owners - step],
                send_sem=row_send.at[k],
                recv_sem=row_recv.at[k],
                device_id=((me + step) % owners, band),
                device_id_type=MESH,
            ).start()
        turned[...] = col_tile[...].T
        edge_cols[k, 0] = turned[pl.ds(1, slots, stride=2), :]
        edge_cols[k, 1] = turned[pl.ds(0, slots, stride=2), :]
        for step in range(4):
            for slot, part, side in ((step, 0, west_band), (4 + step, 1, east_band)):
                pltpu.make_async_remote_copy(
                    src_ref=edge_cols.at[k, part],
                    dst_ref=side_cols.at[k, slot],
                    send_sem=col_send.at[k],
                    recv_sem=col_recv.at[k],
                    device_id=(base + (inner + step) % 4, side),
                    device_id_type=MESH,
                ).start()
        band_rows[k, 0] = edge_rows[k]

    def take(ref, sem):
        pltpu.make_async_copy(ref, ref, sem).wait()

    def build_picks():
        take(band_tables.at[pl.ds(1, owners - 1)], row_recv.at[SWEEPS])
        take(side_tables, col_recv.at[SWEEPS])
        lanes = lax.broadcasted_iota(jnp.int32, (2 * slots, width), 1)
        rows = lax.broadcasted_iota(jnp.int32, (2 * slots, width), 0)
        odd = rows % 2 == 1
        mine = jnp.broadcast_to(table[blocks : blocks + 1, :], (2 * slots, width))
        own = jnp.sum(jnp.where(lanes == rows // 2, mine, 0.0), axis=1, keepdims=True)
        group_ids = ((base + lanes // 8) * bands + band) * blocks + lanes % 8 + 1
        known = (lanes % 8 < blocks) & (lanes < 32)
        match = jnp.where(known & (own == group_ids.astype(jnp.float32)), 1.0, 0.0)
        listed = jnp.concatenate(
            [band_tables[(base + g - me + owners) % owners] for g in range(4)], axis=0
        )
        need = jnp.dot(
            match[:, :32], listed, precision=EXACT, preferred_element_type=jnp.float32
        )
        low = lax.broadcasted_iota(jnp.int32, (8, width), 1) < slots
        per_tile = width // (2 * slots)
        wanted = jnp.where(odd, need[:, 1:2], need[:, 0:1])
        for q in range(owners // per_tile):
            ids = jnp.zeros((8, width), jnp.float32)
            for d in range(per_tile):
                tile = jnp.where(low, band_tables[q * per_tile + d], 0.0)
                twice = tile + pltpu.roll(tile, slots, 1)
                ids = ids + (pltpu.roll(twice, 2 * slots * d, 1) if d else twice)
            id_row = jnp.broadcast_to(ids[blocks : blocks + 1, :], (2 * slots, width))
            bottom = (lanes % (2 * slots)) // slots == 1
            good = (wanted == id_row) & (id_row > 0.0) & (bottom != odd)
            pick_rows[:, q * width : (q + 1) * width] = jnp.where(good, 1.0, 0.0)
        ids = jnp.zeros((8, width), jnp.float32)
        for d in range(8):
            tile = jnp.where(low, side_tables[d], 0.0)
            ids = ids + (pltpu.roll(tile, slots * d, 1) if d else tile)
        id_row = jnp.broadcast_to(ids[blocks : blocks + 1, :], (2 * slots, width))
        western = lanes >= 4 * slots
        for i, (east_of, west_of) in enumerate(((2, 3), (4, 5), (6, 7))):
            wanted = jnp.where(
                odd, need[:, west_of : west_of + 1], need[:, east_of : east_of + 1]
            )
            good = (wanted == id_row) & (id_row > 0.0) & (western == odd)
            pick_cols[2 * slots * i : 2 * slots * (i + 1), :] = jnp.where(good, 1.0, 0.0)

    def take_edges(k):
        now = k % 2
        take(band_rows.at[k, pl.ds(1, owners - 1)], row_recv.at[k])
        per_tile = width // (2 * slots)
        got = jnp.zeros((2 * slots, width), jnp.float32)
        for q in range(owners // per_tile):
            got = got + jnp.dot(
                pick_rows[:, q * width : (q + 1) * width],
                band_rows[k, q * per_tile : (q + 1) * per_tile].reshape(width, width),
                precision=EXACT,
                preferred_element_type=jnp.float32,
            )
        for s in range(slots):
            field[now, s, PAD - 1 : PAD, :] = got[2 * s : 2 * s + 1, :]
            field[now, s, PAD + height : PAD + height + 1, :] = got[2 * s + 1 : 2 * s + 2, :]
        take(side_cols.at[k], col_recv.at[k])
        count = 8 * slots
        cols = jnp.dot(
            pick_cols[:, 0:count],
            side_cols[k].reshape(count, width),
            precision=EXACT,
            preferred_element_type=jnp.float32,
        )
        lanes = lax.broadcasted_iota(jnp.int32, (2 * slots, width), 1)
        straight = cols[0 : 2 * slots]
        above = jnp.where(lanes == width - 1, cols[2 * slots : 4 * slots], straight)
        below = jnp.where(lanes == 0, cols[4 * slots : 6 * slots], straight)
        slanted = pltpu.roll(above, 1, 1) + pltpu.roll(below, width - 1, 1)
        filled = jnp.concatenate(
            [straight, slanted, jnp.zeros((width - 4 * slots, width), jnp.float32)], axis=0
        )
        halo_cols[...] = filled.T

    def around(value, halo):
        left = jnp.where(first_lane, halo, pltpu.roll(value, 1, 1))
        right = jnp.where(last_lane, halo, pltpu.roll(value, width - 1, 1))
        return left + right

    def sweep(k):
        now = k % 2

        def one(s, carry):
            for r0 in range(0, height, CHUNK):
                rows = pl.ds(r0, CHUNK)
                center = field[now, s, pl.ds(PAD + r0, CHUNK), :]
                north = field[now, s, pl.ds(PAD + r0 - 1, CHUNK), :]
                south = field[now, s, pl.ds(PAD + r0 + 1, CHUNK), :]
                vertical = north + south
                cols = halo_cols[rows, :]
                level = around(center, pltpu.roll(cols, width - 1 - 2 * s, 1))
                slant = around(vertical, pltpu.roll(cols, width - 1 - 2 * slots - 2 * s, 1))
                slant = 0.125 * slant
                left = (
                    source[s, rows, :]
                    - coef_d[s, rows, :] * center
                    + coef_x[s, rows, :] * (level + slant)
                    + coef_y[s, rows, :] * (vertical + slant)
                )
                if k == SWEEPS - 1:
                    resid[s, rows, :] = left
                else:
                    weight, keep = weights[k]
                    change = weight * left * inv_d[s, rows, :] + keep * update[s, rows, :]
                    update[s, rows, :] = change
                    fresh = center + change
                    field[1 - now, s, pl.ds(PAD + r0, CHUNK), :] = fresh
                    put_columns(s, r0, fresh)
            return carry

        lax.fori_loop(0, slots, one, 0)

    last = (SWEEPS - 1) % 2

    def rows_of(f, slot, r0, count):
        if f == 0:
            return field[last, slot, pl.ds(PAD + r0, count), :]
        return resid[slot, pl.ds(r0, count), :]

    def start_move(f):
        away = (1 - core) * half

        def fill_half(i, carry):
            slot = find[2 * blocks + i]
            half_out[f, i] = rows_of(f, slot, away, half) * have[2 * blocks + i]
            return carry

        lax.fori_loop(0, 2 * blocks, fill_half, 0)
        pltpu.make_async_remote_copy(
            src_ref=half_out.at[f],
            dst_ref=half_in.at[f],
            send_sem=move_send.at[f, 0],
            recv_sem=move_recv.at[f, 0],
            device_id=(sibling, band),
            device_id_type=MESH,
        ).start()

        def fill_pair(i, carry):
            slot = find[blocks + i]
            pair_out[f, i] = rows_of(f, slot, 0, height) * have[blocks + i]
            return carry

        lax.fori_loop(0, blocks, fill_pair, 0)
        pltpu.make_async_remote_copy(
            src_ref=pair_out.at[f],
            dst_ref=pair_in.at[f],
            send_sem=move_send.at[f, 1],
            recv_sem=move_recv.at[f, 1],
            device_id=(sibling, band),
            device_id_type=MESH,
        ).start()

    def cross_move(f):
        kept = core * half
        take(half_in.at[f], move_recv.at[f, 0])
        for t in range(2):

            def fill(i, carry, t=t):
                slot = find[(2 + t) * blocks + i]
                cross_out[f, t, i] = (
                    rows_of(f, slot, kept, half) * have[(2 + t) * blocks + i]
                    + half_in[f, (1 - t) * blocks + i]
                )
                return carry

            lax.fori_loop(0, blocks, fill, 0)
            pltpu.make_async_remote_copy(
                src_ref=cross_out.at[f, t],
                dst_ref=cross_in.at[f, core],
                send_sem=move_send.at[f, 2 + t],
                recv_sem=move_recv.at[f, 2],
                device_id=(targets[2 + t], band),
                device_id_type=MESH,
            ).start()

    def finish_move(f, out):
        take(pair_in.at[f], move_recv.at[f, 1])

        def near(i, carry):
            out[i] = rows_of(f, find[i], 0, height) * have[i] + pair_in[f, i]
            return carry

        lax.fori_loop(0, blocks, near, 0)
        take(cross_in.at[f], move_recv.at[f, 2])

        def far(i, carry):
            for h in range(2):
                rows = pl.ds(h * half, half)
                out[i, rows, :] = out[i, rows, :] + cross_in[f, h, i]
            return carry

        lax.fori_loop(0, blocks, far, 0)

    pl.semaphore_wait(barrier, owners - 1 + 8)
    send_tables()
    send_edges(0)
    build_picks()
    for k in range(SWEEPS):
        if k == SWEEPS - 1:
            start_move(0)
            cross_move(0)
        take_edges(k)
        sweep(k)
        if k < SWEEPS - 1:
            send_edges(k + 1)
    start_move(1)
    cross_move(1)
    finish_move(0, sol_out)
    finish_move(1, res_out)

    take(band_tables.at[pl.ds(1, owners - 1)], row_send.at[SWEEPS])
    take(side_tables, col_send.at[SWEEPS])
    for k in range(SWEEPS):
        take(band_rows.at[k, pl.ds(1, owners - 1)], row_send.at[k])
        take(side_cols.at[k], col_send.at[k])
    for f in range(2):
        take(half_out.at[f], move_send.at[f, 0])
        take(pair_out.at[f], move_send.at[f, 1])
        take(cross_out.at[f, 0], move_send.at[f, 2])
        take(cross_out.at[f, 1], move_send.at[f, 3])


def per_device(
    owners, bands, depth, cell_dx, cell_dy, forcing, land_mask, dest_block, source_slot, neighbours
):
    slots, height, width = depth.shape
    blocks = source_slot.shape[0]
    half = height // 2
    f32 = jnp.float32
    any_spec = pl.BlockSpec(memory_space=pl.ANY)
    vmem = pl.BlockSpec(memory_space=pltpu.VMEM)
    whole = pltpu.VMEM((slots, height, width), f32)
    dma = pltpu.SemaphoreType.DMA
    out = jax.ShapeDtypeStruct((blocks, height, width), f32)
    return pl.pallas_call(
        functools.partial(kernel, owners, bands),
        out_shape=(out, out),
        in_specs=[any_spec] * 5 + [pl.BlockSpec(memory_space=pltpu.SMEM), vmem, vmem],
        out_specs=(vmem, vmem),
        scratch_shapes=[
            whole,
            whole,
            whole,
            whole,
            pltpu.VMEM((slots, height, width), jnp.int32),
            whole,
            whole,
            whole,
            whole,
            whole,
            whole,
            pltpu.VMEM((2, slots, height + 2 * PAD, width), f32),
            whole,
            pltpu.VMEM((8, width), f32),
            pltpu.VMEM((owners, 8, width), f32),
            pltpu.VMEM((8, 8, width), f32),
            pltpu.VMEM((2 * slots, owners * 2 * slots), f32),
            pltpu.VMEM((6 * slots, width), f32),
            pltpu.VMEM((SWEEPS, 2 * slots, width), f32),
            pltpu.VMEM((SWEEPS, 2, slots, width), f32),
            pltpu.VMEM((SWEEPS, owners, 2 * slots, width), f32),
            pltpu.VMEM((SWEEPS, 8, slots, width), f32),
            pltpu.VMEM((height, width), f32),
            pltpu.VMEM((width, height), f32),
            pltpu.VMEM((height, width), f32),
            pltpu.SMEM((4 * blocks,), jnp.int32),
            pltpu.SMEM((4 * blocks,), f32),
            pltpu.VMEM((2, 2 * blocks, half, width), f32),
            pltpu.VMEM((2, 2 * blocks, half, width), f32),
            pltpu.VMEM((2, blocks, height, width), f32),
            pltpu.VMEM((2, blocks, height, width), f32),
            pltpu.VMEM((2, 2, blocks, half, width), f32),
            pltpu.VMEM((2, 2, blocks, half, width), f32),
            dma((5,)),
            dma((SWEEPS + 1,)),
            dma((SWEEPS + 1,)),
            dma((SWEEPS + 1,)),
            dma((SWEEPS + 1,)),
            dma((2, 4)),
            dma((2, 3)),
        ],
        compiler_params=pltpu.CompilerParams(
            collective_id=0, has_side_effects=True, vmem_limit_bytes=40 * 1024 * 1024
        ),
        name="barotropic_solve",
    )(
        depth,
        cell_dx,
        cell_dy,
        forcing,
        land_mask,
        dest_block,
        dest_block.reshape(1, slots),
        neighbours,
    )


def solution(mesh):
    blocks3 = P(("blk", "grp"), None, None)
    flat = P(("blk", "grp"))
    in_specs = (blocks3,) * 5 + (flat, flat, P(("blk", "grp"), None))
    return jax.shard_map(
        functools.partial(per_device, mesh.shape["blk"], mesh.shape["grp"]),
        mesh=mesh,
        in_specs=in_specs,
        out_specs=(blocks3, blocks3),
        check_vma=False,
    )
```

```python
import functools

import jax
import jax.numpy as jnp
from jax import lax
from jax.experimental import pallas as pl
from jax.experimental.pallas import tpu as pltpu
from jax.sharding import PartitionSpec as P

SWEEPS = 4
TAU_MASS = 6.0
LOW_BOUND = 0.2
HIGH_BOUND = 1.9
CHUNK = 32
PAD = 8
MESH = pl.DeviceIdType.MESH
EXACT = lax.Precision.HIGHEST


def relax_weights():
    alpha = 2.0 / (HIGH_BOUND - LOW_BOUND)
    beta = (HIGH_BOUND + LOW_BOUND) / (HIGH_BOUND - LOW_BOUND)
    gamma = beta / alpha
    weight = 2.0 / gamma
    weights = []
    for _ in range(SWEEPS - 1):
        weight = 1.0 / (gamma - weight / (4.0 * alpha**2))
        weights.append((weight, gamma * weight - 1.0))
    return gamma, weights


def kernel(
    owners,
    bands,
    depth_hbm,
    dx_hbm,
    dy_hbm,
    forcing_hbm,
    mask_hbm,
    dest_smem,
    dest_row,
    neigh,
    sol_out,
    res_out,
    depth_v,
    dx_v,
    dy_v,
    forcing_v,
    mask_v,
    coef_x,
    coef_y,
    coef_d,
    inv_d,
    source,
    update,
    field,
    resid,
    table,
    band_tables,
    side_tables,
    pick_rows,
    pick_cols,
    edge_rows,
    edge_cols,
    band_rows,
    side_cols,
    col_tile,
    row_coefs,
    col_coefs,
    inner_cols,
    filled,
    halo_cols,
    find,
    have,
    half_out,
    half_in,
    pair_out,
    pair_in,
    cross_out,
    cross_in,
    load_sems,
    row_send,
    row_recv,
    col_send,
    col_recv,
    move_send,
    move_recv,
):
    slots, height, width = depth_v.shape
    blocks = neigh.shape[0]
    me = lax.axis_index("blk")
    band = lax.axis_index("grp")
    core = me % 2
    sibling = me + 1 - 2 * core
    base = me - me % 4
    inner = me % 4
    east_band = (band + 1) % bands
    west_band = (band + bands - 1) % bands
    half = height // 2

    loads = [
        pltpu.make_async_copy(src, dst, load_sems.at[i])
        for i, (src, dst) in enumerate(
            (
                (dx_hbm, dx_v),
                (dy_hbm, dy_v),
                (depth_hbm, depth_v),
                (mask_hbm, mask_v),
                (forcing_hbm, forcing_v),
            )
        )
    ]
    for load in loads:
        load.start()

    barrier = pltpu.get_barrier_semaphore()
    for step in range(1, owners):
        pl.semaphore_signal(
            barrier, inc=1, device_id=((me + step) % owners, band), device_id_type=MESH
        )
    for step in range(4):
        for side in (east_band, west_band):
            pl.semaphore_signal(
                barrier,
                inc=1,
                device_id=(base + (inner + step) % 4, side),
                device_id_type=MESH,
            )

    table[...] = jnp.zeros_like(table)
    table[0:blocks, 0:8] = (neigh[...] + 1).astype(jnp.float32)
    table[blocks : blocks + 1, 0:slots] = (dest_row[...] + 1).astype(jnp.float32)
    band_tables[0] = table[...]

    targets = (me, sibling, (base + (inner + 2) % 4), (base + (sibling % 4 + 2) % 4))
    for t, target in enumerate(targets):
        for j in range(blocks):
            wanted = (target * bands + band) * blocks + j
            place = jnp.int32(0)
            count = jnp.int32(0)
            for s in range(slots):
                hit = dest_smem[s] == wanted
                place = jnp.where(hit, s, place)
                count = jnp.where(hit, 1, count)
            find[t * blocks + j] = place
            have[t * blocks + j] = count.astype(jnp.float32)

    gamma, weights = relax_weights()
    lane = lax.broadcasted_iota(jnp.int32, (CHUNK, width), 1)
    first_lane = lane == 0
    last_lane = lane == width - 1

    def put_columns(at, s, r0, value, deep):
        rows = pl.ds(r0, CHUNK)
        right = pltpu.roll(value, at + 1 + deep + s, 1)
        left = pltpu.roll(value, at + slots - deep + s, 1)
        tile = jnp.where(lane == at + s, right, col_tile[rows, :])
        col_tile[rows, :] = jnp.where(lane == at + slots + s, left, tile)

    col_tile[...] = jnp.zeros_like(col_tile)
    for load in loads:
        load.wait()

    def prepare(s, carry):
        for r0 in range(0, height, CHUNK):
            rows = pl.ds(r0, CHUNK)
            ocean = mask_v[s, rows, :].astype(jnp.float32)
            dx = dx_v[s, rows, :]
            dy = dy_v[s, rows, :]
            area = dx * dy
            scaled = depth_v[s, rows, :] * ocean / area
            cx = scaled * (dy * dy)
            cy = scaled * (dx * dx)
            cd = 2.5 * (cx + cy) + TAU_MASS * area
            inv = 1.0 / cd
            src = forcing_v[s, rows, :] * ocean
            start = src * (inv * (1.0 / gamma))
            coef_x[s, rows, :] = cx
            coef_y[s, rows, :] = cy
            coef_d[s, rows, :] = cd
            inv_d[s, rows, :] = inv
            source[s, rows, :] = src
            update[s, rows, :] = start
            field[0, s, pl.ds(PAD + r0, CHUNK), :] = start
            parts = (cx, cy, cd, inv, src, start, start)
            for i, part in enumerate(parts):
                put_columns(2 * slots * i, s, r0, part, 1 if i == 6 else 0)
        return carry

    lax.fori_loop(0, slots, prepare, 0)
    col_coefs[...] = col_tile[...].T
    inner_cols[...] = col_coefs[12 * slots : 14 * slots, :]
    filled[...] = jnp.zeros_like(filled)
    for i, ref in enumerate((coef_x, coef_y, coef_d, inv_d, source, update)):
        for s in range(slots):
            row_coefs[i, s : s + 1, :] = ref[s, 0:1, :]
            row_coefs[i, slots + s : slots + s + 1, :] = ref[s, height - 1 : height, :]
    edge_rows[0] = row_coefs[5]
    edge_cols[0] = col_coefs[10 * slots : 12 * slots, :]

    def send_tables():
        for step in range(1, owners):
            pltpu.make_async_remote_copy(
                src_ref=table,
                dst_ref=band_tables.at[owners - step],
                send_sem=row_send.at[SWEEPS],
                recv_sem=row_recv.at[SWEEPS],
                device_id=((me + step) % owners, band),
                device_id_type=MESH,
            ).start()
        for step in range(4):
            for slot, side in ((step, west_band), (4 + step, east_band)):
                pltpu.make_async_remote_copy(
                    src_ref=table,
                    dst_ref=side_tables.at[slot],
                    send_sem=col_send.at[SWEEPS],
                    recv_sem=col_recv.at[SWEEPS],
                    device_id=(base + (inner + step) % 4, side),
                    device_id_type=MESH,
                ).start()

    def send_edges(k):
        for step in range(1, owners):
            pltpu.make_async_remote_copy(
                src_ref=edge_rows.at[k],
                dst_ref=band_rows.at[k, owners - step],
                send_sem=row_send.at[k],
                recv_sem=row_recv.at[k],
                device_id=((me + step) % owners, band),
                device_id_type=MESH,
            ).start()
        for step in range(4):
            for slot, part, side in ((step, slots, west_band), (4 + step, 0, east_band)):
                pltpu.make_async_remote_copy(
                    src_ref=edge_cols.at[k, pl.ds(part, slots)],
                    dst_ref=side_cols.at[k, slot],
                    send_sem=col_send.at[k],
                    recv_sem=col_recv.at[k],
                    device_id=(base + (inner + step) % 4, side),
                    device_id_type=MESH,
                ).start()
        band_rows[k, 0] = edge_rows[k]

    def take(ref, sem):
        pltpu.make_async_copy(ref, ref, sem).wait()

    def build_picks():
        take(band_tables.at[pl.ds(1, owners - 1)], row_recv.at[SWEEPS])
        take(side_tables, col_recv.at[SWEEPS])
        lanes = lax.broadcasted_iota(jnp.int32, (2 * slots, width), 1)
        rows = lax.broadcasted_iota(jnp.int32, (2 * slots, width), 0)
        lower = rows >= slots
        mine = jnp.broadcast_to(table[blocks : blocks + 1, :], (2 * slots, width))
        own = jnp.sum(jnp.where(lanes == rows % slots, mine, 0.0), axis=1, keepdims=True)
        group_ids = ((base + lanes // 8) * bands + band) * blocks + lanes % 8 + 1
        known = (lanes % 8 < blocks) & (lanes < 32)
        match = jnp.where(known & (own == group_ids.astype(jnp.float32)), 1.0, 0.0)
        listed = jnp.concatenate(
            [band_tables[(base + g - me + owners) % owners] for g in range(4)], axis=0
        )
        need = jnp.dot(
            match[:, :32], listed, precision=EXACT, preferred_element_type=jnp.float32
        )
        low = lax.broadcasted_iota(jnp.int32, (8, width), 1) < slots
        per_tile = width // (2 * slots)
        wanted = jnp.where(lower, need[:, 1:2], need[:, 0:1])
        for q in range(owners // per_tile):
            ids = jnp.zeros((8, width), jnp.float32)
            for d in range(per_tile):
                tile = jnp.where(low, band_tables[q * per_tile + d], 0.0)
                twice = tile + pltpu.roll(tile, slots, 1)
                ids = ids + (pltpu.roll(twice, 2 * slots * d, 1) if d else twice)
            id_row = jnp.broadcast_to(ids[blocks : blocks + 1, :], (2 * slots, width))
            bottom = (lanes % (2 * slots)) // slots == 1
            good = (wanted == id_row) & (id_row > 0.0) & (bottom != lower)
            pick_rows[:, q * width : (q + 1) * width] = jnp.where(good, 1.0, 0.0)
        ids = jnp.zeros((8, width), jnp.float32)
        for d in range(8):
            tile = jnp.where(low, side_tables[d], 0.0)
            ids = ids + (pltpu.roll(tile, slots * d, 1) if d else tile)
        id_row = jnp.broadcast_to(ids[blocks : blocks + 1, :], (2 * slots, width))
        western = lanes >= 4 * slots
        for i, (east_of, west_of) in enumerate(((2, 3), (4, 5), (6, 7))):
            wanted = jnp.where(
                lower, need[:, west_of : west_of + 1], need[:, east_of : east_of + 1]
            )
            good = (wanted == id_row) & (id_row > 0.0) & (western == lower)
            pick_cols[2 * slots * i : 2 * slots * (i + 1), :] = jnp.where(good, 1.0, 0.0)

    def take_edges(k):
        now = k % 2
        take(band_rows.at[k, pl.ds(1, owners - 1)], row_recv.at[k])
        per_tile = width // (2 * slots)
        got = jnp.zeros((2 * slots, width), jnp.float32)
        for q in range(owners // per_tile):
            got = got + jnp.dot(
                pick_rows[:, q * width : (q + 1) * width],
                band_rows[k, q * per_tile : (q + 1) * per_tile].reshape(width, width),
                precision=EXACT,
                preferred_element_type=jnp.float32,
            )
        for s in range(slots):
            field[now, s, PAD - 1 : PAD, :] = got[s : s + 1, :]
            field[now, s, PAD + height : PAD + height + 1, :] = got[slots + s : slots + s + 1, :]
        take(side_cols.at[k], col_recv.at[k])
        count = 8 * slots
        cols = jnp.dot(
            pick_cols[:, 0:count],
            side_cols[k].reshape(count, width),
            precision=EXACT,
            preferred_element_type=jnp.float32,
        )
        lanes = lax.broadcasted_iota(jnp.int32, (2 * slots, width), 1)
        straight = cols[0 : 2 * slots]
        above = jnp.where(lanes == width - 1, cols[2 * slots : 4 * slots], straight)
        below = jnp.where(lanes == 0, cols[4 * slots : 6 * slots], straight)
        slanted = pltpu.roll(above, 1, 1) + pltpu.roll(below, width - 1, 1)
        for i, tile in enumerate((straight, slanted)):
            for h in range(2):
                filled[pl.ds(2 * slots * i + h, slots, stride=2), :] = tile[
                    slots * h : slots * (h + 1)
                ]
        return got, straight, slanted

    def stencil(coefs, center, level, vertical, slant):
        cx, cy, cd, inv, src = (coefs[i] for i in range(5))
        slant = 0.125 * slant
        return (src - cd * center + cx * (level + slant) + cy * (vertical + slant)) * inv

    def ring(k, got, straight, slanted):
        now = k % 2
        weight, keep = weights[k]
        lanes = lax.broadcasted_iota(jnp.int32, (2 * slots, width), 1)
        start = lanes == 0
        end = lanes == width - 1

        def spread(value, before, after):
            left = jnp.where(start, before, pltpu.roll(value, 1, 1))
            return left + jnp.where(end, after, pltpu.roll(value, width - 1, 1))

        def ends(tile, at):
            part = tile[at : at + slots]
            return jnp.concatenate([part[:, 0:1], part[:, width - 1 : width]], axis=0)

        center = edge_rows[k]
        inside = jnp.concatenate(
            [field[now, s, PAD + 1 : PAD + 2, :] for s in range(slots)]
            + [field[now, s, PAD + height - 2 : PAD + height - 1, :] for s in range(slots)],
            axis=0,
        )
        vertical = inside + got
        level = spread(center, ends(straight, slots), ends(straight, 0))
        slant = spread(vertical, ends(slanted, slots), ends(slanted, 0))
        left = stencil([row_coefs[i] for i in range(5)], center, level, vertical, slant)
        change = weight * left + keep * row_coefs[5]
        row_coefs[5] = change
        edge_rows[k + 1] = center + change

        def sides(at, deep):
            part = got[at : at + slots]
            last = width - 1 - deep
            return jnp.concatenate([part[:, last : last + 1], part[:, deep : deep + 1]], axis=0)

        center = edge_cols[k]
        inside = inner_cols[...]
        level = inside + straight
        vertical = spread(center, sides(0, 0), sides(slots, 0))
        slant = slanted + spread(inside, sides(0, 1), sides(slots, 1))
        tall = 2 * slots
        coefs = [col_coefs[i * tall : (i + 1) * tall, :] for i in range(5)]
        left = stencil(coefs, center, level, vertical, slant)
        change = weight * left + keep * col_coefs[5 * tall : 6 * tall, :]
        col_coefs[5 * tall : 6 * tall, :] = change
        edge_cols[k + 1] = center + change

    def around(value, halo):
        left = jnp.where(first_lane, halo, pltpu.roll(value, 1, 1))
        right = jnp.where(last_lane, halo, pltpu.roll(value, width - 1, 1))
        return left + right

    def sweep(k):
        now = k % 2

        def one(s, carry):
            for r0 in range(0, height, CHUNK):
                rows = pl.ds(r0, CHUNK)
                center = field[now, s, pl.ds(PAD + r0, CHUNK), :]
                north = field[now, s, pl.ds(PAD + r0 - 1, CHUNK), :]
                south = field[now, s, pl.ds(PAD + r0 + 1, CHUNK), :]
                vertical = north + south
                cols = halo_cols[rows, :]
                level = around(center, pltpu.roll(cols, width - 1 - 2 * s, 1))
                slant = around(vertical, pltpu.roll(cols, width - 1 - 2 * slots - 2 * s, 1))
                slant = 0.125 * slant
                left = (
                    source[s, rows, :]
                    - coef_d[s, rows, :] * center
                    + coef_x[s, rows, :] * (level + slant)
                    + coef_y[s, rows, :] * (vertical + slant)
                )
                if k == SWEEPS - 1:
                    resid[s, rows, :] = left
                else:
                    weight, keep = weights[k]
                    change = weight * left * inv_d[s, rows, :] + keep * update[s, rows, :]
                    update[s, rows, :] = change
                    fresh = center + change
                    field[1 - now, s, pl.ds(PAD + r0, CHUNK), :] = fresh
                    put_columns(0, s, r0, fresh, 1)
            return carry

        halo_cols[...] = filled[...].T
        lax.fori_loop(0, slots, one, 0)
        if k < SWEEPS - 1:
            inner_cols[...] = col_tile[...].T[0 : 2 * slots]

    last = (SWEEPS - 1) % 2

    def rows_of(f, slot, r0, count):
        if f == 0:
            return field[last, slot, pl.ds(PAD + r0, count), :]
        return resid[slot, pl.ds(r0, count), :]

    def start_move(f):
        away = (1 - core) * half

        def fill_half(i, carry):
            slot = find[2 * blocks + i]
            half_out[f, i] = rows_of(f, slot, away, half) * have[2 * blocks + i]
            return carry

        lax.fori_loop(0, 2 * blocks, fill_half, 0)
        pltpu.make_async_remote_copy(
            src_ref=half_out.at[f],
            dst_ref=half_in.at[f],
            send_sem=move_send.at[f, 0],
            recv_sem=move_recv.at[f, 0],
            device_id=(sibling, band),
            device_id_type=MESH,
        ).start()

        def fill_pair(i, carry):
            slot = find[blocks + i]
            pair_out[f, i] = rows_of(f, slot, 0, height) * have[blocks + i]
            return carry

        lax.fori_loop(0, blocks, fill_pair, 0)
        pltpu.make_async_remote_copy(
            src_ref=pair_out.at[f],
            dst_ref=pair_in.at[f],
            send_sem=move_send.at[f, 1],
            recv_sem=move_recv.at[f, 1],
            device_id=(sibling, band),
            device_id_type=MESH,
        ).start()

    def cross_move(f):
        kept = core * half
        take(half_in.at[f], move_recv.at[f, 0])
        for t in range(2):

            def fill(i, carry, t=t):
                slot = find[(2 + t) * blocks + i]
                cross_out[f, t, i] = (
                    rows_of(f, slot, kept, half) * have[(2 + t) * blocks + i]
                    + half_in[f, (1 - t) * blocks + i]
                )
                return carry

            lax.fori_loop(0, blocks, fill, 0)
            pltpu.make_async_remote_copy(
                src_ref=cross_out.at[f, t],
                dst_ref=cross_in.at[f, core],
                send_sem=move_send.at[f, 2 + t],
                recv_sem=move_recv.at[f, 2],
                device_id=(targets[2 + t], band),
                device_id_type=MESH,
            ).start()

    def finish_move(f, out):
        take(pair_in.at[f], move_recv.at[f, 1])

        def near(i, carry):
            out[i] = rows_of(f, find[i], 0, height) * have[i] + pair_in[f, i]
            return carry

        lax.fori_loop(0, blocks, near, 0)
        take(cross_in.at[f], move_recv.at[f, 2])

        def far(i, carry):
            for h in range(2):
                rows = pl.ds(h * half, half)
                out[i, rows, :] = out[i, rows, :] + cross_in[f, h, i]
            return carry

        lax.fori_loop(0, blocks, far, 0)

    pl.semaphore_wait(barrier, owners - 1 + 8)
    send_tables()
    send_edges(0)
    build_picks()
    for k in range(SWEEPS):
        if k == SWEEPS - 1:
            start_move(0)
            cross_move(0)
        halo = take_edges(k)
        if k < SWEEPS - 1:
            ring(k, *halo)
            send_edges(k + 1)
        sweep(k)
    start_move(1)
    cross_move(1)
    finish_move(0, sol_out)
    finish_move(1, res_out)

    take(band_tables.at[pl.ds(1, owners - 1)], row_send.at[SWEEPS])
    take(side_tables, col_send.at[SWEEPS])
    for k in range(SWEEPS):
        take(band_rows.at[k, pl.ds(1, owners - 1)], row_send.at[k])
        take(side_cols.at[k], col_send.at[k])
    for f in range(2):
        take(half_out.at[f], move_send.at[f, 0])
        take(pair_out.at[f], move_send.at[f, 1])
        take(cross_out.at[f, 0], move_send.at[f, 2])
        take(cross_out.at[f, 1], move_send.at[f, 3])


def per_device(
    owners, bands, depth, cell_dx, cell_dy, forcing, land_mask, dest_block, source_slot, neighbours
):
    slots, height, width = depth.shape
    blocks = source_slot.shape[0]
    half = height // 2
    f32 = jnp.float32
    any_spec = pl.BlockSpec(memory_space=pl.ANY)
    vmem = pl.BlockSpec(memory_space=pltpu.VMEM)
    whole = pltpu.VMEM((slots, height, width), f32)
    dma = pltpu.SemaphoreType.DMA
    out = jax.ShapeDtypeStruct((blocks, height, width), f32)
    return pl.pallas_call(
        functools.partial(kernel, owners, bands),
        out_shape=(out, out),
        in_specs=[any_spec] * 5 + [pl.BlockSpec(memory_space=pltpu.SMEM), vmem, vmem],
        out_specs=(vmem, vmem),
        scratch_shapes=[
            whole,
            whole,
            whole,
            whole,
            pltpu.VMEM((slots, height, width), jnp.int32),
            whole,
            whole,
            whole,
            whole,
            whole,
            whole,
            pltpu.VMEM((2, slots, height + 2 * PAD, width), f32),
            whole,
            pltpu.VMEM((8, width), f32),
            pltpu.VMEM((owners, 8, width), f32),
            pltpu.VMEM((8, 8, width), f32),
            pltpu.VMEM((2 * slots, owners * 2 * slots), f32),
            pltpu.VMEM((6 * slots, width), f32),
            pltpu.VMEM((SWEEPS, 2 * slots, width), f32),
            pltpu.VMEM((SWEEPS, 2 * slots, width), f32),
            pltpu.VMEM((SWEEPS, owners, 2 * slots, width), f32),
            pltpu.VMEM((SWEEPS, 8, slots, width), f32),
            pltpu.VMEM((height, width), f32),
            pltpu.VMEM((6, 2 * slots, width), f32),
            pltpu.VMEM((width, height), f32),
            pltpu.VMEM((2 * slots, width), f32),
            pltpu.VMEM((width, height), f32),
            pltpu.VMEM((height, width), f32),
            pltpu.SMEM((4 * blocks,), jnp.int32),
            pltpu.SMEM((4 * blocks,), f32),
            pltpu.VMEM((2, 2 * blocks, half, width), f32),
            pltpu.VMEM((2, 2 * blocks, half, width), f32),
            pltpu.VMEM((2, blocks, height, width), f32),
            pltpu.VMEM((2, blocks, height, width), f32),
            pltpu.VMEM((2, 2, blocks, half, width), f32),
            pltpu.VMEM((2, 2, blocks, half, width), f32),
            dma((5,)),
            dma((SWEEPS + 1,)),
            dma((SWEEPS + 1,)),
            dma((SWEEPS + 1,)),
            dma((SWEEPS + 1,)),
            dma((2, 4)),
            dma((2, 3)),
        ],
        compiler_params=pltpu.CompilerParams(
            collective_id=0, has_side_effects=True, vmem_limit_bytes=60 * 1024 * 1024
        ),
        name="barotropic_solve",
    )(
        depth,
        cell_dx,
        cell_dy,
        forcing,
        land_mask,
        dest_block,
        dest_block.reshape(1, slots),
        neighbours,
    )


def solution(mesh):
    blocks3 = P(("blk", "grp"), None, None)
    flat = P(("blk", "grp"))
    in_specs = (blocks3,) * 5 + (flat, flat, P(("blk", "grp"), None))
    return jax.shard_map(
        functools.partial(per_device, mesh.shape["blk"], mesh.shape["grp"]),
        mesh=mesh,
        in_specs=in_specs,
        out_specs=(blocks3, blocks3),
        check_vma=False,
    )
```

```python
import functools

import jax
import jax.numpy as jnp
from jax import lax
from jax.experimental import pallas as pl
from jax.experimental.pallas import tpu as pltpu
from jax.sharding import PartitionSpec as P

SWEEPS = 4
TAU_MASS = 6.0
LOW_BOUND = 0.2
HIGH_BOUND = 1.9
CHUNK = 32
PAD = 8
MESH = pl.DeviceIdType.MESH
EXACT = lax.Precision.HIGHEST


def relax_weights():
    alpha = 2.0 / (HIGH_BOUND - LOW_BOUND)
    beta = (HIGH_BOUND + LOW_BOUND) / (HIGH_BOUND - LOW_BOUND)
    gamma = beta / alpha
    weight = 2.0 / gamma
    weights = []
    for _ in range(SWEEPS - 1):
        weight = 1.0 / (gamma - weight / (4.0 * alpha**2))
        weights.append((weight, gamma * weight - 1.0))
    return gamma, weights


def kernel(
    owners,
    bands,
    depth_hbm,
    dx_hbm,
    dy_hbm,
    forcing_hbm,
    mask_hbm,
    dest_smem,
    dest_row,
    neigh,
    sol_out,
    res_out,
    depth_v,
    dx_v,
    dy_v,
    forcing_v,
    mask_v,
    coef_x,
    coef_y,
    coef_d,
    inv_d,
    source,
    update,
    field,
    resid,
    table,
    band_tables,
    side_tables,
    pick_rows,
    pick_cols,
    edge_rows,
    edge_cols,
    band_rows,
    side_cols,
    col_tile,
    row_coefs,
    col_coefs,
    inner_cols,
    filled,
    halo_cols,
    find,
    have,
    half_out,
    half_in,
    pair_out,
    pair_in,
    cross_out,
    cross_in,
    load_sems,
    row_send,
    row_recv,
    col_send,
    col_recv,
    move_send,
    move_recv,
):
    slots, height, width = depth_v.shape
    blocks = neigh.shape[0]
    me = lax.axis_index("blk")
    band = lax.axis_index("grp")
    core = me % 2
    sibling = me + 1 - 2 * core
    base = me - me % 4
    inner = me % 4
    east_band = (band + 1) % bands
    west_band = (band + bands - 1) % bands
    half = height // 2

    loads = [
        pltpu.make_async_copy(src, dst, load_sems.at[i])
        for i, (src, dst) in enumerate(
            (
                (dx_hbm, dx_v),
                (dy_hbm, dy_v),
                (depth_hbm, depth_v),
                (mask_hbm, mask_v),
                (forcing_hbm, forcing_v),
            )
        )
    ]
    for load in loads:
        load.start()

    barrier = pltpu.get_barrier_semaphore()
    for step in range(4):
        for side in (east_band, west_band):
            pl.semaphore_signal(
                barrier,
                inc=1,
                device_id=(base + (inner + step) % 4, side),
                device_id_type=MESH,
            )
    for step in range(1, owners):
        pl.semaphore_signal(
            barrier, inc=1, device_id=((me + step) % owners, band), device_id_type=MESH
        )

    table[...] = jnp.zeros_like(table)
    table[0:blocks, 0:8] = (neigh[...] + 1).astype(jnp.float32)
    table[blocks : blocks + 1, 0:slots] = (dest_row[...] + 1).astype(jnp.float32)
    band_tables[0] = table[...]

    targets = (me, sibling, (base + (inner + 2) % 4), (base + (sibling % 4 + 2) % 4))
    for t, target in enumerate(targets):
        for j in range(blocks):
            wanted = (target * bands + band) * blocks + j
            place = jnp.int32(0)
            count = jnp.int32(0)
            for s in range(slots):
                hit = dest_smem[s] == wanted
                place = jnp.where(hit, s, place)
                count = jnp.where(hit, 1, count)
            find[t * blocks + j] = place
            have[t * blocks + j] = count.astype(jnp.float32)

    gamma, weights = relax_weights()
    lane = lax.broadcasted_iota(jnp.int32, (CHUNK, width), 1)
    first_lane = lane == 0
    last_lane = lane == width - 1

    def put_columns(at, s, r0, value, deep):
        rows = pl.ds(r0, CHUNK)
        right = pltpu.roll(value, at + 1 + deep + s, 1)
        left = pltpu.roll(value, at + slots - deep + s, 1)
        tile = jnp.where(lane == at + s, right, col_tile[rows, :])
        col_tile[rows, :] = jnp.where(lane == at + slots + s, left, tile)

    col_tile[...] = jnp.zeros_like(col_tile)
    for load in loads:
        load.wait()

    def prepare(s, carry):
        for r0 in range(0, height, CHUNK):
            rows = pl.ds(r0, CHUNK)
            ocean = mask_v[s, rows, :].astype(jnp.float32)
            dx = dx_v[s, rows, :]
            dy = dy_v[s, rows, :]
            area = dx * dy
            scaled = depth_v[s, rows, :] * ocean / area
            cx = scaled * (dy * dy)
            cy = scaled * (dx * dx)
            cd = 2.5 * (cx + cy) + TAU_MASS * area
            inv = 1.0 / cd
            src = forcing_v[s, rows, :] * ocean
            start = src * (inv * (1.0 / gamma))
            coef_x[s, rows, :] = cx
            coef_y[s, rows, :] = cy
            coef_d[s, rows, :] = cd
            inv_d[s, rows, :] = inv
            source[s, rows, :] = src
            update[s, rows, :] = start
            field[0, s, pl.ds(PAD + r0, CHUNK), :] = start
            parts = (cx, cy, cd, inv, src, start, start)
            for i, part in enumerate(parts):
                put_columns(2 * slots * i, s, r0, part, 1 if i == 6 else 0)
        return carry

    lax.fori_loop(0, slots, prepare, 0)
    col_coefs[...] = col_tile[...].T
    inner_cols[...] = col_coefs[12 * slots : 14 * slots, :]
    filled[...] = jnp.zeros_like(filled)
    for i, ref in enumerate((coef_x, coef_y, coef_d, inv_d, source, update)):
        for s in range(slots):
            row_coefs[i, s : s + 1, :] = ref[s, 0:1, :]
            row_coefs[i, slots + s : slots + s + 1, :] = ref[s, height - 1 : height, :]
    edge_rows[0] = row_coefs[5]
    edge_cols[0] = col_coefs[10 * slots : 12 * slots, :]

    def send_tables():
        for step in range(4):
            for slot, side in ((step, west_band), (4 + step, east_band)):
                pltpu.make_async_remote_copy(
                    src_ref=table,
                    dst_ref=side_tables.at[slot],
                    send_sem=col_send.at[SWEEPS],
                    recv_sem=col_recv.at[SWEEPS],
                    device_id=(base + (inner + step) % 4, side),
                    device_id_type=MESH,
                ).start()
        for step in range(1, owners):
            pltpu.make_async_remote_copy(
                src_ref=table,
                dst_ref=band_tables.at[owners - step],
                send_sem=row_send.at[SWEEPS],
                recv_sem=row_recv.at[SWEEPS],
                device_id=((me + step) % owners, band),
                device_id_type=MESH,
            ).start()

    def send_cols(k):
        for step in range(4):
            for slot, part, side in ((step, slots, west_band), (4 + step, 0, east_band)):
                pltpu.make_async_remote_copy(
                    src_ref=edge_cols.at[k, pl.ds(part, slots)],
                    dst_ref=side_cols.at[k, slot],
                    send_sem=col_send.at[k],
                    recv_sem=col_recv.at[k],
                    device_id=(base + (inner + step) % 4, side),
                    device_id_type=MESH,
                ).start()

    def send_rows(k):
        for step in range(1, owners):
            pltpu.make_async_remote_copy(
                src_ref=edge_rows.at[k],
                dst_ref=band_rows.at[k, owners - step],
                send_sem=row_send.at[k],
                recv_sem=row_recv.at[k],
                device_id=((me + step) % owners, band),
                device_id_type=MESH,
            ).start()
        band_rows[k, 0] = edge_rows[k]

    def take(ref, sem):
        pltpu.make_async_copy(ref, ref, sem).wait()

    def build_picks():
        take(band_tables.at[pl.ds(1, owners - 1)], row_recv.at[SWEEPS])
        take(side_tables, col_recv.at[SWEEPS])
        lanes = lax.broadcasted_iota(jnp.int32, (2 * slots, width), 1)
        rows = lax.broadcasted_iota(jnp.int32, (2 * slots, width), 0)
        lower = rows >= slots
        mine = jnp.broadcast_to(table[blocks : blocks + 1, :], (2 * slots, width))
        own = jnp.sum(jnp.where(lanes == rows % slots, mine, 0.0), axis=1, keepdims=True)
        group_ids = ((base + lanes // 8) * bands + band) * blocks + lanes % 8 + 1
        known = (lanes % 8 < blocks) & (lanes < 32)
        match = jnp.where(known & (own == group_ids.astype(jnp.float32)), 1.0, 0.0)
        listed = jnp.concatenate(
            [band_tables[(base + g - me + owners) % owners] for g in range(4)], axis=0
        )
        need = jnp.dot(
            match[:, :32], listed, precision=EXACT, preferred_element_type=jnp.float32
        )
        low = lax.broadcasted_iota(jnp.int32, (8, width), 1) < slots
        per_tile = width // (2 * slots)
        wanted = jnp.where(lower, need[:, 1:2], need[:, 0:1])
        for q in range(owners // per_tile):
            ids = jnp.zeros((8, width), jnp.float32)
            for d in range(per_tile):
                tile = jnp.where(low, band_tables[q * per_tile + d], 0.0)
                twice = tile + pltpu.roll(tile, slots, 1)
                ids = ids + (pltpu.roll(twice, 2 * slots * d, 1) if d else twice)
            id_row = jnp.broadcast_to(ids[blocks : blocks + 1, :], (2 * slots, width))
            bottom = (lanes % (2 * slots)) // slots == 1
            good = (wanted == id_row) & (id_row > 0.0) & (bottom != lower)
            pick_rows[:, q * width : (q + 1) * width] = jnp.where(good, 1.0, 0.0)
        ids = jnp.zeros((8, width), jnp.float32)
        for d in range(8):
            tile = jnp.where(low, side_tables[d], 0.0)
            ids = ids + (pltpu.roll(tile, slots * d, 1) if d else tile)
        id_row = jnp.broadcast_to(ids[blocks : blocks + 1, :], (2 * slots, width))
        western = lanes >= 4 * slots
        for i, (east_of, west_of) in enumerate(((2, 3), (4, 5), (6, 7))):
            wanted = jnp.where(
                lower, need[:, west_of : west_of + 1], need[:, east_of : east_of + 1]
            )
            good = (wanted == id_row) & (id_row > 0.0) & (western == lower)
            pick_cols[2 * slots * i : 2 * slots * (i + 1), :] = jnp.where(good, 1.0, 0.0)

    def take_edges(k):
        take(band_rows.at[k, pl.ds(1, owners - 1)], row_recv.at[k])
        per_tile = width // (2 * slots)
        got = jnp.zeros((2 * slots, width), jnp.float32)
        for q in range(owners // per_tile):
            got = got + jnp.dot(
                pick_rows[:, q * width : (q + 1) * width],
                band_rows[k, q * per_tile : (q + 1) * per_tile].reshape(width, width),
                precision=EXACT,
                preferred_element_type=jnp.float32,
            )
        take(side_cols.at[k], col_recv.at[k])
        count = 8 * slots
        cols = jnp.dot(
            pick_cols[:, 0:count],
            side_cols[k].reshape(count, width),
            precision=EXACT,
            preferred_element_type=jnp.float32,
        )
        lanes = lax.broadcasted_iota(jnp.int32, (2 * slots, width), 1)
        straight = cols[0 : 2 * slots]
        above = jnp.where(lanes == width - 1, cols[2 * slots : 4 * slots], straight)
        below = jnp.where(lanes == 0, cols[4 * slots : 6 * slots], straight)
        slanted = pltpu.roll(above, 1, 1) + pltpu.roll(below, width - 1, 1)
        return got, straight, slanted

    def put_halo(k, got, straight, slanted):
        now = k % 2
        for s in range(slots):
            field[now, s, PAD - 1 : PAD, :] = got[s : s + 1, :]
            field[now, s, PAD + height : PAD + height + 1, :] = got[slots + s : slots + s + 1, :]
        for i, tile in enumerate((straight, slanted)):
            for h in range(2):
                filled[pl.ds(2 * slots * i + h, slots, stride=2), :] = tile[
                    slots * h : slots * (h + 1)
                ]
        halo_cols[...] = filled[...].T

    def stencil(coefs, center, level, vertical, slant):
        cx, cy, cd, inv, src = (coefs[i] for i in range(5))
        slant = 0.125 * slant
        return (src - cd * center + cx * (level + slant) + cy * (vertical + slant)) * inv

    def ring(k, got, straight, slanted):
        now = k % 2
        weight, keep = weights[k]
        lanes = lax.broadcasted_iota(jnp.int32, (2 * slots, width), 1)
        start = lanes == 0
        end = lanes == width - 1

        def spread(value, before, after):
            left = jnp.where(start, before, pltpu.roll(value, 1, 1))
            return left + jnp.where(end, after, pltpu.roll(value, width - 1, 1))

        def ends(tile, at):
            part = tile[at : at + slots]
            return jnp.concatenate([part[:, 0:1], part[:, width - 1 : width]], axis=0)

        def sides(at, deep):
            part = got[at : at + slots]
            last = width - 1 - deep
            return jnp.concatenate([part[:, last : last + 1], part[:, deep : deep + 1]], axis=0)

        center = edge_cols[k]
        inside = inner_cols[...]
        level = inside + straight
        vertical = spread(center, sides(0, 0), sides(slots, 0))
        slant = slanted + spread(inside, sides(0, 1), sides(slots, 1))
        tall = 2 * slots
        coefs = [col_coefs[i * tall : (i + 1) * tall, :] for i in range(5)]
        left = stencil(coefs, center, level, vertical, slant)
        change = weight * left + keep * col_coefs[5 * tall : 6 * tall, :]
        col_coefs[5 * tall : 6 * tall, :] = change
        edge_cols[k + 1] = center + change
        send_cols(k + 1)

        center = edge_rows[k]
        inside = jnp.concatenate(
            [field[now, s, PAD + 1 : PAD + 2, :] for s in range(slots)]
            + [field[now, s, PAD + height - 2 : PAD + height - 1, :] for s in range(slots)],
            axis=0,
        )
        vertical = inside + got
        level = spread(center, ends(straight, slots), ends(straight, 0))
        slant = spread(vertical, ends(slanted, slots), ends(slanted, 0))
        left = stencil([row_coefs[i] for i in range(5)], center, level, vertical, slant)
        change = weight * left + keep * row_coefs[5]
        row_coefs[5] = change
        edge_rows[k + 1] = center + change
        send_rows(k + 1)

    def around(value, halo):
        left = jnp.where(first_lane, halo, pltpu.roll(value, 1, 1))
        right = jnp.where(last_lane, halo, pltpu.roll(value, width - 1, 1))
        return left + right

    def sweep(k, first, stop):
        now = k % 2

        def one(s, carry):
            for r0 in range(0, height, CHUNK):
                rows = pl.ds(r0, CHUNK)
                center = field[now, s, pl.ds(PAD + r0, CHUNK), :]
                north = field[now, s, pl.ds(PAD + r0 - 1, CHUNK), :]
                south = field[now, s, pl.ds(PAD + r0 + 1, CHUNK), :]
                vertical = north + south
                cols = halo_cols[rows, :]
                level = around(center, pltpu.roll(cols, width - 1 - 2 * s, 1))
                slant = around(vertical, pltpu.roll(cols, width - 1 - 2 * slots - 2 * s, 1))
                slant = 0.125 * slant
                left = (
                    source[s, rows, :]
                    - coef_d[s, rows, :] * center
                    + coef_x[s, rows, :] * (level + slant)
                    + coef_y[s, rows, :] * (vertical + slant)
                )
                if k == SWEEPS - 1:
                    resid[s, rows, :] = left
                else:
                    weight, keep = weights[k]
                    change = weight * left * inv_d[s, rows, :] + keep * update[s, rows, :]
                    update[s, rows, :] = change
                    fresh = center + change
                    field[1 - now, s, pl.ds(PAD + r0, CHUNK), :] = fresh
                    put_columns(0, s, r0, fresh, 1)
            return carry

        lax.fori_loop(first, stop, one, 0)
        if k < SWEEPS - 1:
            inner_cols[...] = col_tile[...].T[0 : 2 * slots]

    last = (SWEEPS - 1) % 2

    def rows_of(f, slot, r0, count):
        if f == 0:
            return field[last, slot, pl.ds(PAD + r0, count), :]
        return resid[slot, pl.ds(r0, count), :]

    def start_move(f):
        away = (1 - core) * half

        def fill_half(i, carry):
            slot = find[2 * blocks + i]
            half_out[f, i] = rows_of(f, slot, away, half) * have[2 * blocks + i]
            return carry

        lax.fori_loop(0, 2 * blocks, fill_half, 0)
        pltpu.make_async_remote_copy(
            src_ref=half_out.at[f],
            dst_ref=half_in.at[f],
            send_sem=move_send.at[f, 0],
            recv_sem=move_recv.at[f, 0],
            device_id=(sibling, band),
            device_id_type=MESH,
        ).start()

        def fill_pair(i, carry):
            slot = find[blocks + i]
            pair_out[f, i] = rows_of(f, slot, 0, height) * have[blocks + i]
            return carry

        lax.fori_loop(0, blocks, fill_pair, 0)
        pltpu.make_async_remote_copy(
            src_ref=pair_out.at[f],
            dst_ref=pair_in.at[f],
            send_sem=move_send.at[f, 1],
            recv_sem=move_recv.at[f, 1],
            device_id=(sibling, band),
            device_id_type=MESH,
        ).start()

    def cross_move(f):
        kept = core * half
        take(half_in.at[f], move_recv.at[f, 0])
        for t in range(2):

            def fill(i, carry, t=t):
                slot = find[(2 + t) * blocks + i]
                cross_out[f, t, i] = (
                    rows_of(f, slot, kept, half) * have[(2 + t) * blocks + i]
                    + half_in[f, (1 - t) * blocks + i]
                )
                return carry

            lax.fori_loop(0, blocks, fill, 0)
            pltpu.make_async_remote_copy(
                src_ref=cross_out.at[f, t],
                dst_ref=cross_in.at[f, core],
                send_sem=move_send.at[f, 2 + t],
                recv_sem=move_recv.at[f, 2],
                device_id=(targets[2 + t], band),
                device_id_type=MESH,
            ).start()

    def finish_move(f, out):
        take(pair_in.at[f], move_recv.at[f, 1])

        def near(i, carry):
            out[i] = rows_of(f, find[i], 0, height) * have[i] + pair_in[f, i]
            return carry

        lax.fori_loop(0, blocks, near, 0)
        take(cross_in.at[f], move_recv.at[f, 2])

        def far(i, carry):
            for h in range(2):
                rows = pl.ds(h * half, half)
                out[i, rows, :] = out[i, rows, :] + cross_in[f, h, i]
            return carry

        lax.fori_loop(0, blocks, far, 0)

    pl.semaphore_wait(barrier, owners - 1 + 8)
    send_tables()
    send_cols(0)
    send_rows(0)
    build_picks()
    for k in range(SWEEPS - 1):
        halo = take_edges(k)
        ring(k, *halo)
        put_halo(k, *halo)
        sweep(k, 0, slots)
    start_move(0)
    cross_move(0)
    put_halo(SWEEPS - 1, *take_edges(SWEEPS - 1))
    sweep(SWEEPS - 1, 0, slots)
    start_move(1)
    cross_move(1)
    finish_move(0, sol_out)
    finish_move(1, res_out)

    take(band_tables.at[pl.ds(1, owners - 1)], row_send.at[SWEEPS])
    take(side_tables, col_send.at[SWEEPS])
    for k in range(SWEEPS):
        take(band_rows.at[k, pl.ds(1, owners - 1)], row_send.at[k])
        take(side_cols.at[k], col_send.at[k])
    for f in range(2):
        take(half_out.at[f], move_send.at[f, 0])
        take(pair_out.at[f], move_send.at[f, 1])
        take(cross_out.at[f, 0], move_send.at[f, 2])
        take(cross_out.at[f, 1], move_send.at[f, 3])


def per_device(
    owners, bands, depth, cell_dx, cell_dy, forcing, land_mask, dest_block, source_slot, neighbours
):
    slots, height, width = depth.shape
    blocks = source_slot.shape[0]
    half = height // 2
    f32 = jnp.float32
    any_spec = pl.BlockSpec(memory_space=pl.ANY)
    vmem = pl.BlockSpec(memory_space=pltpu.VMEM)
    whole = pltpu.VMEM((slots, height, width), f32)
    dma = pltpu.SemaphoreType.DMA
    out = jax.ShapeDtypeStruct((blocks, height, width), f32)
    return pl.pallas_call(
        functools.partial(kernel, owners, bands),
        out_shape=(out, out),
        in_specs=[any_spec] * 5 + [pl.BlockSpec(memory_space=pltpu.SMEM), vmem, vmem],
        out_specs=(vmem, vmem),
        scratch_shapes=[
            whole,
            whole,
            whole,
            whole,
            pltpu.VMEM((slots, height, width), jnp.int32),
            whole,
            whole,
            whole,
            whole,
            whole,
            whole,
            pltpu.VMEM((2, slots, height + 2 * PAD, width), f32),
            whole,
            pltpu.VMEM((8, width), f32),
            pltpu.VMEM((owners, 8, width), f32),
            pltpu.VMEM((8, 8, width), f32),
            pltpu.VMEM((2 * slots, owners * 2 * slots), f32),
            pltpu.VMEM((6 * slots, width), f32),
            pltpu.VMEM((SWEEPS, 2 * slots, width), f32),
            pltpu.VMEM((SWEEPS, 2 * slots, width), f32),
            pltpu.VMEM((SWEEPS, owners, 2 * slots, width), f32),
            pltpu.VMEM((SWEEPS, 8, slots, width), f32),
            pltpu.VMEM((height, width), f32),
            pltpu.VMEM((6, 2 * slots, width), f32),
            pltpu.VMEM((width, height), f32),
            pltpu.VMEM((2 * slots, width), f32),
            pltpu.VMEM((width, height), f32),
            pltpu.VMEM((height, width), f32),
            pltpu.SMEM((4 * blocks,), jnp.int32),
            pltpu.SMEM((4 * blocks,), f32),
            pltpu.VMEM((2, 2 * blocks, half, width), f32),
            pltpu.VMEM((2, 2 * blocks, half, width), f32),
            pltpu.VMEM((2, blocks, height, width), f32),
            pltpu.VMEM((2, blocks, height, width), f32),
            pltpu.VMEM((2, 2, blocks, half, width), f32),
            pltpu.VMEM((2, 2, blocks, half, width), f32),
            dma((5,)),
            dma((SWEEPS + 1,)),
            dma((SWEEPS + 1,)),
            dma((SWEEPS + 1,)),
            dma((SWEEPS + 1,)),
            dma((2, 4)),
            dma((2, 3)),
        ],
        compiler_params=pltpu.CompilerParams(
            collective_id=0, has_side_effects=True, vmem_limit_bytes=60 * 1024 * 1024
        ),
        name="barotropic_solve",
    )(
        depth,
        cell_dx,
        cell_dy,
        forcing,
        land_mask,
        dest_block,
        dest_block.reshape(1, slots),
        neighbours,
    )


def solution(mesh):
    blocks3 = P(("blk", "grp"), None, None)
    flat = P(("blk", "grp"))
    in_specs = (blocks3,) * 5 + (flat, flat, P(("blk", "grp"), None))
    return jax.shard_map(
        functools.partial(per_device, mesh.shape["blk"], mesh.shape["grp"]),
        mesh=mesh,
        in_specs=in_specs,
        out_specs=(blocks3, blocks3),
        check_vma=False,
    )
```
